32 devices in a mesh: inst: 4 (over y, x), row: 2 (over core), pitch: 4 (over z).
Axes of the slice: x: 2, y: 2, z: 4, core: 2. Of those that a mesh axis runs over, the one named last changes fastest.
Arguments:
- direction: float32 [4, 5, 12288], P('inst', None, ('row', 'pitch')), may hold values from -6 to 6
- time_matrix: float32 [4, 4], replicated, may hold values from -3 to 3
- volume: float32 [12288], P(('row', 'pitch')), may hold values from 0.5 to 2
- diag_jac: float32 [4, 25, 12288], P('inst', None, ('row', 'pitch')), may hold values from -2.5 to 2.5
- face_jac: float32 [4, 50, 24576], P('inst', None, ('row', 'pitch')), may hold values from -1 to 1
- face_left: int32 [24576], P(('row', 'pitch')), may hold values from 0 to 1535
- face_right: int32 [24576], P(('row', 'pitch')), may hold values from 0 to 1535
- bound_jac: float32 [4, 4, 50, 3072], P('inst', None, None, ('row', 'pitch')), may hold values from -1 to 1
- bound_cell: int32 [4, 3072], P(None, ('row', 'pitch')), may hold values from 0 to 1535
- send_cell: int32 [4, 3072], P(None, ('row', 'pitch')), may hold values from 0 to 1535
Outputs:
- product: float32 [4, 5, 12288], P('inst', None, ('row', 'pitch'))
The draws below stay inside these ranges and needn't reach their ends.
Inputs may be any that keep to these rules, and one draw needn't show every extreme that they name: `face_left`: a cell index local to the face's block of 1536 cells. `face_right`: a cell index local to the face's block of 1536 cells. `bound_cell`: a cell index local to the face's block of 1536 cells. `send_cell`: a cell index local to the supplying block of 1536 cells.
All inputs are finite; a program needn't handle non-finite values.
Results may differ from the reference program's by a relative error of at most 0.000052.
Values sent between devices are 32-bit elements; how exact they have to be, the bound alone decides.
A program may use at most 128 MiB of HBM per device.

```python
import math
import jax
import jax.numpy as jnp
from jax import lax

CELL_DEV = 1536
NT = 4
COMP = 5
FACE_DEV = 3072
BND_DEV = 384
CELLS = 12288
FACES = 24576
BOUNDS = 3072
N_ROW = 2
N_PITCH = 4


def plant(values, stream_key, smallest, largest):
    shape = values.shape
    place = [jax.random.randint(jax.random.fold_in(stream_key, axis), (), 0, shape[axis]) for axis in range(len(shape))]
    values = values.at[tuple(place)].set(smallest)
    longest = shape.index(max(shape))
    place[longest] = (place[longest] + 1) % shape[longest]
    return values.at[tuple(place)].set(largest)


def block_levels(own_key, shape, cuts, least, top_value):
    level = 1.0
    for axis_at, parts in cuts:
        draws = jax.random.uniform(jax.random.fold_in(jax.random.fold_in(own_key, 6), axis_at), (parts,), jnp.float32, least / len(cuts), top_value / len(cuts))
        level = level * jnp.repeat(jnp.exp(draws), shape[axis_at] // parts).reshape((-1,) + (1,) * (len(shape) - 1 - axis_at))
    return level


def bell_draw(own_key, shape, width, limit, pieces=(), kind=jnp.bfloat16):
    values = width * jax.random.normal(own_key, shape, jnp.float32)
    if pieces:
        values = values * block_levels(own_key, shape, pieces, -0.22, 0.18)
    return jnp.clip(values, -limit, limit).astype(kind)


def setup_inputs(seed: int = 0) -> dict:
    streams_of = jax.random.split(jax.random.key(seed), 11)
    return {
        "direction": bell_draw(streams_of[0], (NT, COMP, CELLS), 1.0, 6.0, ((0, 4), (2, 8)), jnp.float32),
        "time_matrix": bell_draw(streams_of[1], (NT, NT), NT ** -0.5, 3.0, (), jnp.float32),
        "volume": jnp.clip(jnp.exp(math.log(2.0) - 1.3862944 * jax.random.uniform(streams_of[2], (CELLS,), jnp.float32) ** block_levels(streams_of[2], (CELLS,), ((0, 8),), -0.2, 0.2)), 0.5, 2.0),
        "diag_jac": bell_draw(streams_of[3], (NT, COMP * COMP, CELLS), 5 ** -0.5, 2.5, ((0, 4), (2, 8)), jnp.float32),
        "face_jac": bell_draw(streams_of[4], (NT, 2 * COMP * COMP, FACES), 30 ** -0.5, 1.0, ((0, 4), (2, 8)), jnp.float32),
        "face_left": plant(jax.random.randint(streams_of[5], (FACES,), 0, CELL_DEV), jax.random.fold_in(streams_of[5], 1), 0, CELL_DEV - 1).astype(jnp.int32),
        "face_right": plant(jax.random.randint(streams_of[6], (FACES,), 0, CELL_DEV), jax.random.fold_in(streams_of[6], 1), 0, CELL_DEV - 1).astype(jnp.int32),
        "bound_jac": bell_draw(streams_of[7], (NT, 4, 2 * COMP * COMP, BOUNDS), 30 ** -0.5, 1.0, ((0, 4), (3, 8)), jnp.float32),
        "bound_cell": plant(jax.random.randint(streams_of[8], (4, BOUNDS), 0, CELL_DEV), jax.random.fold_in(streams_of[8], 1), 0, CELL_DEV - 1).astype(jnp.int32),
        "send_cell": plant(jax.random.randint(streams_of[9], (4, BOUNDS), 0, CELL_DEV), jax.random.fold_in(streams_of[9], 1), 0, CELL_DEV - 1).astype(jnp.int32),
    }


def reference(direction, time_matrix, volume, diag_jac, face_jac, face_left, face_right, bound_jac, bound_cell, send_cell):
    high = lax.Precision.HIGHEST
    spectral = jnp.einsum('ij,jcx->icx', time_matrix, direction, precision=high) * volume[None, None, :]
    blocks = diag_jac.reshape(NT, 5, 5, CELLS)
    result = spectral + jnp.einsum('tabx,tbx->tax', blocks, direction, precision=high)
    offset = (jnp.arange(FACES, dtype=jnp.int32) // FACE_DEV) * CELL_DEV
    left_cell = (face_left + offset).astype(jnp.int32)
    right_cell = (face_right + offset).astype(jnp.int32)
    pair = face_jac.reshape(NT, 2, 5, 5, FACES)
    flux = jnp.einsum('tabf,tbf->taf', pair[:, 0], direction[:, :, left_cell], precision=high)
    flux = flux + jnp.einsum('tabf,tbf->taf', pair[:, 1], direction[:, :, right_cell], precision=high)
    result = result.at[:, :, left_cell].add(flux).at[:, :, right_cell].add(-flux)
    bound_offset = (jnp.arange(BOUNDS, dtype=jnp.int32) // BND_DEV) * CELL_DEV
    own_cell = (bound_cell + bound_offset[None, :]).astype(jnp.int32)
    sent_cell = (send_cell + bound_offset[None, :]).astype(jnp.int32)
    sent = direction[:, :, sent_cell].reshape(NT, 5, 4, N_ROW, N_PITCH, BND_DEV)
    ghost_low = jnp.roll(sent[:, :, 1], 1, axis=3)
    ghost_high = jnp.roll(sent[:, :, 0], -1, axis=3)
    zero_rim = jnp.zeros((NT, 5, 1, N_PITCH, BND_DEV), jnp.float32)
    ghost_below = jnp.concatenate([zero_rim, sent[:, :, 3][:, :, :-1]], axis=2)
    ghost_above = jnp.concatenate([sent[:, :, 2][:, :, 1:], zero_rim], axis=2)
    ghosts = jnp.stack([ghost_low, ghost_high, ghost_below, ghost_above], axis=2).reshape(NT, 5, 4, BOUNDS)
    inner = direction[:, :, own_cell]
    bound_pair = bound_jac.reshape(NT, 4, 2, 5, 5, BOUNDS)
    bound_flux = jnp.einsum('tkabx,tbkx->takx', bound_pair[:, :, 0], inner, precision=high)
    bound_flux = bound_flux + jnp.einsum('tkabx,tbkx->takx', bound_pair[:, :, 1], ghosts, precision=high)
    result = result.at[:, :, own_cell.reshape(-1)].add(bound_flux.reshape(NT, 5, 4 * BOUNDS))
    return result
```

```python
import functools
import jax
import jax.numpy as jnp
from jax import lax
from jax.experimental import pallas as pl
from jax.experimental.pallas import tpu as pltpu
from jax.sharding import PartitionSpec as P

LANE = 128
COMP = 5
TERMS = 2 * COMP
PACK = 16
GROUP = 4
MESH = pl.DeviceIdType.MESH


def gathered(own, cell):
    low = cell & (LANE - 1)
    high = cell >> 7
    chunks = own.shape[1] * GROUP
    masks = [high == h for h in range(chunks)]
    values = []
    for b in range(COMP):
        found = None
        for h in range(chunks):
            row = own[b, h // GROUP, pl.ds(h % GROUP, 1), :]
            part = jnp.take_along_axis(
                jnp.broadcast_to(row, cell.shape), low, axis=1, mode="promise_in_bounds"
            )
            found = part if h == 0 else jnp.where(masks[h], part, found)
        values.append(found)
    return values


def applied(block, base, values):
    result = []
    for a in range(COMP):
        total = None
        for b in range(COMP):
            term = block(base + COMP * a + b) * values[b]
            total = term if total is None else total + term
        result.append(total)
    return result


def two_terms(value):
    first = value.astype(jnp.bfloat16).astype(jnp.float32)
    return first, value - first


def packed_row(row):
    return jnp.broadcast_to(row, (PACK, LANE)).astype(jnp.bfloat16)


def hot_tile(hot, place, cell_row, value):
    low = packed_row((cell_row & (LANE - 1)).astype(jnp.float32))
    for s in range(0, LANE, PACK):
        index = lax.broadcasted_iota(jnp.int32, (PACK, LANE), 0) + s
        index = index.astype(jnp.float32).astype(jnp.bfloat16)
        hot[s : s + PACK, place : place + LANE] = jnp.where(
            index == low, jnp.bfloat16(value), jnp.bfloat16(0)
        )


def chunk_mask(cell_row):
    index = lax.broadcasted_iota(jnp.int32, (PACK, LANE), 0)
    index = index.astype(jnp.float32).astype(jnp.bfloat16)
    return index == packed_row((cell_row >> 7).astype(jnp.float32))


def kernel(
    n_inst,
    n_row,
    n_pitch,
    tm_ref,
    dir_hbm,
    vol_hbm,
    diag_hbm,
    face_hbm,
    left_hbm,
    right_hbm,
    bound_hbm,
    bcell_hbm,
    scell_hbm,
    out_ref,
    own,
    vol_line,
    vol,
    diag,
    face,
    left,
    right,
    bound,
    bcell,
    scell,
    dirs,
    ghost_out,
    ghost_in,
    flux_terms,
    bound_terms,
    rows,
    hot,
    acc,
    local_sem,
    inst_send,
    inst_recv,
    ghost_send,
    ghost_recv,
):
    t = lax.axis_index("inst")
    r = lax.axis_index("row")
    p = lax.axis_index("pitch")
    blocks = own.shape[1]
    chunks = blocks * GROUP
    f_tiles = left.shape[0]
    faces = f_tiles * LANE
    bounds = bcell.shape[1]
    b_tiles = bounds // LANE

    pairs = [
        (dir_hbm, own),
        (scell_hbm, scell),
        (bcell_hbm, bcell),
        (left_hbm, left),
        (right_hbm, right),
        (face_hbm, face),
        (bound_hbm, bound),
        (diag_hbm, diag),
        (vol_hbm, vol_line),
    ]
    copies = [
        pltpu.make_async_copy(a, b, local_sem.at[i]) for i, (a, b) in enumerate(pairs)
    ]
    for c in copies:
        c.start()

    barrier = pltpu.get_barrier_semaphore()

    def greet(**place):
        pl.semaphore_signal(barrier, inc=1, device_id=place, device_id_type=MESH)

    for o in range(1, n_inst):
        greet(inst=lax.rem(t + o, n_inst))
    up = lax.rem(p + 1, n_pitch)
    down = lax.rem(p + n_pitch - 1, n_pitch)
    greet(pitch=up)
    greet(pitch=down)

    @pl.when(r > 0)
    def _():
        greet(row=r - 1)

    @pl.when(r < n_row - 1)
    def _():
        greet(row=r + 1)

    for c in copies[0:3]:
        c.wait()
    inner = []
    for j in range(b_tiles):
        at = slice(j * LANE, (j + 1) * LANE)
        values = gathered(own, jnp.concatenate([scell[:, at], bcell[:, at]], axis=0))
        for b in range(COMP):
            ghost_out[j, pl.ds(b, GROUP, stride=8), :] = values[b][0:GROUP]
        inner.append([v[GROUP : 2 * GROUP] for v in values])

    greeted = 2 + n_inst - 1
    extra = jnp.where(r > 0, 1, 0) + jnp.where(r < n_row - 1, 1, 0)
    pl.semaphore_wait(barrier, greeted + extra)

    def ghost_copy(k, **place):
        opposite = k ^ 1
        return pltpu.make_async_remote_copy(
            src_ref=ghost_out.at[:, 8 * k : 8 * k + 8],
            dst_ref=ghost_in.at[:, 8 * opposite : 8 * opposite + 8],
            send_sem=ghost_send.at[k],
            recv_sem=ghost_recv.at[opposite],
            device_id=place,
            device_id_type=MESH,
        )

    to_down = ghost_copy(0, pitch=down)
    to_up = ghost_copy(1, pitch=up)
    to_down.start()
    to_up.start()

    @pl.when(r > 0)
    def _():
        ghost_copy(2, row=r - 1).start()

    @pl.when(r < n_row - 1)
    def _():
        ghost_copy(3, row=r + 1).start()

    sends = []
    for o in range(1, n_inst):
        c = pltpu.make_async_remote_copy(
            src_ref=dir_hbm,
            dst_ref=dirs.at[o],
            send_sem=inst_send.at[o],
            recv_sem=inst_recv.at[o],
            device_id={"inst": lax.rem(t + o, n_inst)},
            device_id_type=MESH,
        )
        c.start()
        sends.append(c)

    @pl.when(r == 0)
    def _():
        ghost_in[:, 16:24, :] = jnp.zeros((b_tiles, 8, LANE), jnp.float32)

    @pl.when(r == n_row - 1)
    def _():
        ghost_in[:, 24:32, :] = jnp.zeros((b_tiles, 8, LANE), jnp.float32)

    for c in copies[3:9]:
        c.wait()

    def product(start, size):
        return lax.dot_general(
            rows[:, start : start + size],
            hot[:, start : start + size],
            (((1,), (1,)), ((), ())),
            preferred_element_type=jnp.float32,
        )

    total = None
    for g in range(0, f_tiles, 8):
        block = lambda i, g=g: face[i, g : g + 8, :]
        cell_l = left[g : g + 8, :]
        cell_r = right[g : g + 8, :]
        one = applied(block, 0, gathered(own, cell_l))
        two = applied(block, COMP * COMP, gathered(own, cell_r))
        for a in range(COMP):
            first, rest = two_terms(one[a] + two[a])
            flux_terms[a, g : g + 8, :] = first
            flux_terms[COMP + a, g : g + 8, :] = rest
        for s in range(g, g + 8):
            place = 2 * s * LANE
            row_l = left[s : s + 1, :]
            row_r = right[s : s + 1, :]
            hot_tile(hot, place, row_l, 1.0)
            hot_tile(hot, place + LANE, row_r, -1.0)
            mask_l = chunk_mask(row_l)
            mask_r = chunk_mask(row_r)
            for a in range(TERMS):
                value = packed_row(flux_terms[a, s : s + 1, :])
                at = slice(a * PACK, (a + 1) * PACK)
                zero = jnp.bfloat16(0)
                rows[at, place : place + LANE] = jnp.where(mask_l, value, zero)
                rows[at, place + LANE : place + 2 * LANE] = jnp.where(mask_r, value, zero)
        part = product(2 * g * LANE, 16 * LANE)
        total = part if total is None else total + part
    acc[...] = total

    inner_flux = []
    for j in range(b_tiles):
        at = slice(j * LANE, (j + 1) * LANE)
        inner_flux.append(applied(lambda i, at=at: bound[i, :, at], 0, inner[j]))
        for k in range(GROUP):
            hot_tile(hot, 2 * faces + (j * GROUP + k) * LANE, bcell[k : k + 1, at], 1.0)
    for h in range(chunks):
        vol[h // GROUP, pl.ds(h % GROUP, 1), :] = vol_line[
            h * LANE : (h + 1) * LANE
        ].reshape(1, LANE)

    to_down.wait()
    to_up.wait()

    @pl.when(r > 0)
    def _():
        ghost_copy(2, row=r - 1).wait_send()
        half = ghost_in.at[:, 16:24]
        pltpu.make_async_copy(half, half, ghost_recv.at[2]).wait()

    @pl.when(r < n_row - 1)
    def _():
        ghost_copy(3, row=r + 1).wait_send()
        half = ghost_in.at[:, 24:32]
        pltpu.make_async_copy(half, half, ghost_recv.at[3]).wait()

    for j in range(b_tiles):
        at = slice(j * LANE, (j + 1) * LANE)
        outer = [ghost_in[j, pl.ds(b, GROUP, stride=8), :] for b in range(COMP)]
        flux = applied(lambda i, at=at: bound[i, :, at], COMP * COMP, outer)
        for a in range(COMP):
            first, rest = two_terms(inner_flux[j][a] + flux[a])
            bound_terms[a, j] = first
            bound_terms[COMP + a, j] = rest
        for k in range(GROUP):
            place = 2 * faces + (j * GROUP + k) * LANE
            mask = chunk_mask(bcell[k : k + 1, at])
            for a in range(TERMS):
                value = packed_row(bound_terms[a, j, pl.ds(k, 1), :])
                rows[a * PACK : (a + 1) * PACK, place : place + LANE] = jnp.where(
                    mask, value, jnp.bfloat16(0)
                )
    acc[...] = acc[...] + product(2 * faces, 4 * bounds)

    for c in sends:
        c.wait()
    for q in range(blocks):
        mine = [own[b, q] for b in range(COMP)]
        local = applied(lambda i, q=q: diag[i, q], 0, mine)
        for a in range(COMP):
            mixed = tm_ref[t, t] * mine[a]
            for o in range(1, n_inst):
                mixed = mixed + tm_ref[t, lax.rem(t + n_inst - o, n_inst)] * dirs[o, a, q]
            at = a * PACK + q * GROUP
            both = acc[at : at + GROUP, :]
            at = at + COMP * PACK
            both = both + acc[at : at + GROUP, :]
            out_ref[a, q] = mixed * vol[q] + local[a] + both


def per_device(
    direction,
    time_matrix,
    volume,
    diag_jac,
    face_jac,
    face_left,
    face_right,
    bound_jac,
    bound_cell,
    send_cell,
):
    n_inst = lax.axis_size("inst")
    n_row = lax.axis_size("row")
    n_pitch = lax.axis_size("pitch")
    cells = direction.shape[2]
    faces = face_left.shape[0]
    bounds = bound_cell.shape[1]
    blocks = cells // (GROUP * LANE)
    f_tiles = faces // LANE
    b_tiles = bounds // LANE
    width = 2 * faces + 4 * bounds
    f32, i32, bf16 = jnp.float32, jnp.int32, jnp.bfloat16
    cell_view = (blocks, GROUP, LANE)
    hbm = pl.BlockSpec(memory_space=pl.ANY)
    result = pl.pallas_call(
        functools.partial(kernel, n_inst, n_row, n_pitch),
        out_shape=jax.ShapeDtypeStruct((COMP, *cell_view), f32),
        in_specs=[pl.BlockSpec(memory_space=pltpu.SMEM)] + [hbm] * 9,
        out_specs=pl.BlockSpec(memory_space=pltpu.VMEM),
        scratch_shapes=[
            pltpu.VMEM((COMP, *cell_view), f32),
            pltpu.VMEM((cells,), f32),
            pltpu.VMEM(cell_view, f32),
            pltpu.VMEM((25, *cell_view), f32),
            pltpu.VMEM((50, f_tiles, LANE), f32),
            pltpu.VMEM((f_tiles, LANE), i32),
            pltpu.VMEM((f_tiles, LANE), i32),
            pltpu.VMEM((50, 4, bounds), f32),
            pltpu.VMEM((4, bounds), i32),
            pltpu.VMEM((4, bounds), i32),
            pltpu.VMEM((n_inst, COMP, *cell_view), f32),
            pltpu.VMEM((b_tiles, 32, LANE), f32),
            pltpu.VMEM((b_tiles, 32, LANE), f32),
            pltpu.VMEM((TERMS, f_tiles, LANE), f32),
            pltpu.VMEM((TERMS, b_tiles, GROUP, LANE), f32),
            pltpu.VMEM((TERMS * PACK, width), bf16),
            pltpu.VMEM((LANE, width), bf16),
            pltpu.VMEM((TERMS * PACK, LANE), f32),
            pltpu.SemaphoreType.DMA((9,)),
            pltpu.SemaphoreType.DMA((n_inst,)),
            pltpu.SemaphoreType.DMA((n_inst,)),
            pltpu.SemaphoreType.DMA((4,)),
            pltpu.SemaphoreType.DMA((4,)),
        ],
        compiler_params=pltpu.CompilerParams(collective_id=0, has_side_effects=True),
    )(
        time_matrix,
        direction[0].reshape(COMP, *cell_view),
        volume,
        diag_jac[0].reshape(25, *cell_view),
        face_jac[0].reshape(50, f_tiles, LANE),
        face_left.reshape(f_tiles, LANE),
        face_right.reshape(f_tiles, LANE),
        bound_jac[0].transpose(1, 0, 2),
        bound_cell,
        send_cell,
    )
    return result.reshape(1, COMP, cells)


def solution(mesh):
    return jax.shard_map(
        per_device,
        mesh=mesh,
        in_specs=(
            P("inst", None, ("row", "pitch")),
            P(),
            P(("row", "pitch")),
            P("inst", None, ("row", "pitch")),
            P("inst", None, ("row", "pitch")),
            P(("row", "pitch")),
            P(("row", "pitch")),
            P("inst", None, None, ("row", "pitch")),
            P(None, ("row", "pitch")),
            P(None, ("row", "pitch")),
        ),
        out_specs=P("inst", None, ("row", "pitch")),
        check_vma=False,
    )
```

```python
import functools
import jax
import jax.numpy as jnp
from jax import lax
from jax.experimental import pallas as pl
from jax.experimental.pallas import tpu as pltpu
from jax.sharding import PartitionSpec as P

LANE = 128
COMP = 5
TERMS = 2 * COMP
PACK = 16
GROUP = 4
MESH = pl.DeviceIdType.MESH


def gathered(own, cell):
    low = cell & (LANE - 1)
    high = cell >> 7
    chunks = own.shape[1] * GROUP
    masks = [high == h for h in range(chunks)]
    values = []
    for b in range(COMP):
        found = None
        for h in range(chunks):
            row = own[b, h // GROUP, pl.ds(h % GROUP, 1), :]
            part = jnp.take_along_axis(
                jnp.broadcast_to(row, cell.shape), low, axis=1, mode="promise_in_bounds"
            )
            found = part if h == 0 else jnp.where(masks[h], part, found)
        values.append(found)
    return values


def applied(block, base, values):
    result = []
    for a in range(COMP):
        total = None
        for b in range(COMP):
            term = block(base + COMP * a + b) * values[b]
            total = term if total is None else total + term
        result.append(total)
    return result


def two_terms(value):
    first = value.astype(jnp.bfloat16).astype(jnp.float32)
    return first, value - first


def packed_row(row):
    return jnp.broadcast_to(row, (PACK, LANE)).astype(jnp.bfloat16)


def hot_tile(hot, place, cell_row, value):
    low = packed_row((cell_row & (LANE - 1)).astype(jnp.float32))
    for s in range(0, LANE, PACK):
        index = lax.broadcasted_iota(jnp.int32, (PACK, LANE), 0) + s
        index = index.astype(jnp.float32).astype(jnp.bfloat16)
        hot[s : s + PACK, place : place + LANE] = jnp.where(
            index == low, jnp.bfloat16(value), jnp.bfloat16(0)
        )


def chunk_mask(cell_row):
    index = lax.broadcasted_iota(jnp.int32, (PACK, LANE), 0)
    index = index.astype(jnp.float32).astype(jnp.bfloat16)
    return index == packed_row((cell_row >> 7).astype(jnp.float32))


def kernel(
    n_inst,
    n_row,
    n_pitch,
    tm_hbm,
    dir_hbm,
    vol_hbm,
    diag_hbm,
    face_hbm,
    left_hbm,
    right_hbm,
    bound_hbm,
    bcell_hbm,
    scell_hbm,
    out_ref,
    tm_ref,
    own,
    vol_line,
    vol,
    diag,
    face,
    left,
    right,
    bound,
    bcell,
    scell,
    dirs,
    ghost_out,
    ghost_in,
    flux_terms,
    bound_terms,
    rows,
    hot,
    acc,
    local_sem,
    inst_send,
    inst_recv,
    ghost_send,
    ghost_recv,
):
    t = lax.axis_index("inst")
    r = lax.axis_index("row")
    p = lax.axis_index("pitch")
    blocks = own.shape[1]
    chunks = blocks * GROUP
    f_tiles = left.shape[0]
    faces = f_tiles * LANE
    bounds = bcell.shape[1]
    b_tiles = bounds // LANE

    barrier = pltpu.get_barrier_semaphore()

    def greet(**place):
        pl.semaphore_signal(barrier, inc=1, device_id=place, device_id_type=MESH)

    up = lax.rem(p + 1, n_pitch)
    down = lax.rem(p + n_pitch - 1, n_pitch)
    greet(pitch=up)
    greet(pitch=down)

    @pl.when(r > 0)
    def _():
        greet(row=r - 1)

    @pl.when(r < n_row - 1)
    def _():
        greet(row=r + 1)

    for o in range(1, n_inst):
        greet(inst=lax.rem(t + o, n_inst))

    pairs = [
        (dir_hbm, own),
        (scell_hbm, scell),
        (bcell_hbm, bcell),
        (left_hbm, left),
        (right_hbm, right),
        (face_hbm, face),
        (bound_hbm, bound),
        (diag_hbm, diag),
        (vol_hbm, vol_line),
        (tm_hbm, tm_ref),
    ]
    copies = [
        pltpu.make_async_copy(a, b, local_sem.at[i]) for i, (a, b) in enumerate(pairs)
    ]
    for c in copies:
        c.start()

    for c in copies[0:3]:
        c.wait()
    inner = []
    for j in range(b_tiles):
        at = slice(j * LANE, (j + 1) * LANE)
        values = gathered(own, jnp.concatenate([scell[:, at], bcell[:, at]], axis=0))
        for b in range(COMP):
            ghost_out[j, pl.ds(b, GROUP, stride=8), :] = values[b][0:GROUP]
        inner.append([v[GROUP : 2 * GROUP] for v in values])

    greeted = 2 + n_inst - 1
    extra = jnp.where(r > 0, 1, 0) + jnp.where(r < n_row - 1, 1, 0)
    pl.semaphore_wait(barrier, greeted + extra)

    def ghost_copy(k, **place):
        opposite = k ^ 1
        return pltpu.make_async_remote_copy(
            src_ref=ghost_out.at[:, 8 * k : 8 * k + COMP],
            dst_ref=ghost_in.at[:, 8 * opposite : 8 * opposite + COMP],
            send_sem=ghost_send.at[k],
            recv_sem=ghost_recv.at[opposite],
            device_id=place,
            device_id_type=MESH,
        )

    to_down = ghost_copy(0, pitch=down)
    to_up = ghost_copy(1, pitch=up)
    to_down.start()
    to_up.start()

    @pl.when(r > 0)
    def _():
        ghost_copy(2, row=r - 1).start()

    @pl.when(r < n_row - 1)
    def _():
        ghost_copy(3, row=r + 1).start()

    sends = []
    for o in range(1, n_inst):
        c = pltpu.make_async_remote_copy(
            src_ref=dir_hbm,
            dst_ref=dirs.at[o],
            send_sem=inst_send.at[o],
            recv_sem=inst_recv.at[o],
            device_id={"inst": lax.rem(t + o, n_inst)},
            device_id_type=MESH,
        )
        c.start()
        sends.append(c)

    @pl.when(r == 0)
    def _():
        ghost_in[:, 16:24, :] = jnp.zeros((b_tiles, 8, LANE), jnp.float32)

    @pl.when(r == n_row - 1)
    def _():
        ghost_in[:, 24:32, :] = jnp.zeros((b_tiles, 8, LANE), jnp.float32)

    for c in copies[3:10]:
        c.wait()

    def product(start, size):
        return lax.dot_general(
            rows[:, start : start + size],
            hot[:, start : start + size],
            (((1,), (1,)), ((), ())),
            preferred_element_type=jnp.float32,
        )

    total = None
    for g in range(0, f_tiles, 8):
        block = lambda i, g=g: face[i, g : g + 8, :]
        cell_l = left[g : g + 8, :]
        cell_r = right[g : g + 8, :]
        one = applied(block, 0, gathered(own, cell_l))
        two = applied(block, COMP * COMP, gathered(own, cell_r))
        for a in range(COMP):
            first, rest = two_terms(one[a] + two[a])
            flux_terms[a, g : g + 8, :] = first
            flux_terms[COMP + a, g : g + 8, :] = rest
        for s in range(g, g + 8):
            place = 2 * s * LANE
            row_l = left[s : s + 1, :]
            row_r = right[s : s + 1, :]
            hot_tile(hot, place, row_l, 1.0)
            hot_tile(hot, place + LANE, row_r, -1.0)
            mask_l = chunk_mask(row_l)
            mask_r = chunk_mask(row_r)
            for a in range(TERMS):
                value = packed_row(flux_terms[a, s : s + 1, :])
                at = slice(a * PACK, (a + 1) * PACK)
                zero = jnp.bfloat16(0)
                rows[at, place : place + LANE] = jnp.where(mask_l, value, zero)
                rows[at, place + LANE : place + 2 * LANE] = jnp.where(mask_r, value, zero)
        part = product(2 * g * LANE, 16 * LANE)
        total = part if total is None else total + part
    acc[...] = total

    def boundary_place(j, k):
        pair = 1 - k // 2
        return 2 * faces + 2 * pair * bounds + (2 * j + k % 2) * LANE

    inner_flux = []
    for j in range(b_tiles):
        at = slice(j * LANE, (j + 1) * LANE)
        inner_flux.append(applied(lambda i, at=at: bound[i, :, at], 0, inner[j]))
        for k in range(GROUP):
            hot_tile(hot, boundary_place(j, k), bcell[k : k + 1, at], 1.0)
    for h in range(chunks):
        vol[h // GROUP, pl.ds(h % GROUP, 1), :] = vol_line[
            h * LANE : (h + 1) * LANE
        ].reshape(1, LANE)

    for c in sends:
        c.wait()
    for q in range(blocks):
        mine = [own[b, q] for b in range(COMP)]
        local = applied(lambda i, q=q: diag[i, q], 0, mine)
        for a in range(COMP):
            mixed = tm_ref[t, t] * mine[a]
            for o in range(1, n_inst):
                mixed = mixed + tm_ref[t, lax.rem(t + n_inst - o, n_inst)] * dirs[o, a, q]
            out_ref[a, q] = mixed * vol[q] + local[a]

    def boundary(start):
        for j in range(b_tiles):
            at = slice(j * LANE, (j + 1) * LANE)
            outer = [
                ghost_in[j, pl.ds(8 * start + b, 2, stride=8), :] for b in range(COMP)
            ]
            block = lambda i, at=at: bound[i, start : start + 2, at]
            flux = applied(block, COMP * COMP, outer)
            for a in range(COMP):
                first, rest = two_terms(inner_flux[j][a][start : start + 2] + flux[a])
                bound_terms[a, j, start : start + 2, :] = first
                bound_terms[COMP + a, j, start : start + 2, :] = rest
            for k in range(start, start + 2):
                place = boundary_place(j, k)
                mask = chunk_mask(bcell[k : k + 1, at])
                for a in range(TERMS):
                    value = packed_row(bound_terms[a, j, pl.ds(k, 1), :])
                    rows[a * PACK : (a + 1) * PACK, place : place + LANE] = jnp.where(
                        mask, value, jnp.bfloat16(0)
                    )

    @pl.when(r > 0)
    def _():
        ghost_copy(2, row=r - 1).wait_send()
        half = ghost_in.at[:, 16 : 16 + COMP]
        pltpu.make_async_copy(half, half, ghost_recv.at[2]).wait()

    @pl.when(r < n_row - 1)
    def _():
        ghost_copy(3, row=r + 1).wait_send()
        half = ghost_in.at[:, 24 : 24 + COMP]
        pltpu.make_async_copy(half, half, ghost_recv.at[3]).wait()

    boundary(2)
    acc[...] = acc[...] + product(2 * faces, 2 * bounds)

    to_down.wait()
    to_up.wait()
    boundary(0)
    acc[...] = acc[...] + product(2 * faces + 2 * bounds, 2 * bounds)
    for q in range(blocks):
        for a in range(COMP):
            at = a * PACK + q * GROUP
            both = acc[at : at + GROUP, :]
            at = at + COMP * PACK
            out_ref[a, q] = out_ref[a, q] + (both + acc[at : at + GROUP, :])


def per_device(
    direction,
    time_matrix,
    volume,
    diag_jac,
    face_jac,
    face_left,
    face_right,
    bound_jac,
    bound_cell,
    send_cell,
):
    n_inst = lax.axis_size("inst")
    n_row = lax.axis_size("row")
    n_pitch = lax.axis_size("pitch")
    cells = direction.shape[2]
    faces = face_left.shape[0]
    bounds = bound_cell.shape[1]
    blocks = cells // (GROUP * LANE)
    f_tiles = faces // LANE
    b_tiles = bounds // LANE
    width = 2 * faces + 4 * bounds
    f32, i32, bf16 = jnp.float32, jnp.int32, jnp.bfloat16
    cell_view = (blocks, GROUP, LANE)
    hbm = pl.BlockSpec(memory_space=pl.ANY)
    result = pl.pallas_call(
        functools.partial(kernel, n_inst, n_row, n_pitch),
        out_shape=pltpu.VMEM((COMP, *cell_view), f32),
        in_specs=[hbm] * 10,
        out_specs=pl.BlockSpec(memory_space=pltpu.VMEM),
        scratch_shapes=[
            pltpu.SMEM((n_inst, n_inst), f32),
            pltpu.VMEM((COMP, *cell_view), f32),
            pltpu.VMEM((cells,), f32),
            pltpu.VMEM(cell_view, f32),
            pltpu.VMEM((25, *cell_view), f32),
            pltpu.VMEM((50, f_tiles, LANE), f32),
            pltpu.VMEM((f_tiles, LANE), i32),
            pltpu.VMEM((f_tiles, LANE), i32),
            pltpu.VMEM((50, 4, bounds), f32),
            pltpu.VMEM((4, bounds), i32),
            pltpu.VMEM((4, bounds), i32),
            pltpu.VMEM((n_inst, COMP, *cell_view), f32),
            pltpu.VMEM((b_tiles, 32, LANE), f32),
            pltpu.VMEM((b_tiles, 32, LANE), f32),
            pltpu.VMEM((TERMS, f_tiles, LANE), f32),
            pltpu.VMEM((TERMS, b_tiles, GROUP, LANE), f32),
            pltpu.VMEM((TERMS * PACK, width), bf16),
            pltpu.VMEM((LANE, width), bf16),
            pltpu.VMEM((TERMS * PACK, LANE), f32),
            pltpu.SemaphoreType.DMA((10,)),
            pltpu.SemaphoreType.DMA((n_inst,)),
            pltpu.SemaphoreType.DMA((n_inst,)),
            pltpu.SemaphoreType.DMA((4,)),
            pltpu.SemaphoreType.DMA((4,)),
        ],
        compiler_params=pltpu.CompilerParams(collective_id=0, has_side_effects=True),
    )(
        time_matrix,
        direction[0].reshape(COMP, *cell_view),
        volume,
        diag_jac[0].reshape(25, *cell_view),
        face_jac[0].reshape(50, f_tiles, LANE),
        face_left.reshape(f_tiles, LANE),
        face_right.reshape(f_tiles, LANE),
        bound_jac[0].transpose(1, 0, 2),
        bound_cell,
        send_cell,
    )
    return result.reshape(1, COMP, cells)


def solution(mesh):
    return jax.shard_map(
        per_device,
        mesh=mesh,
        in_specs=(
            P("inst", None, ("row", "pitch")),
            P(),
            P(("row", "pitch")),
            P("inst", None, ("row", "pitch")),
            P("inst", None, ("row", "pitch")),
            P(("row", "pitch")),
            P(("row", "pitch")),
            P("inst", None, None, ("row", "pitch")),
            P(None, ("row", "pitch")),
            P(None, ("row", "pitch")),
        ),
        out_specs=P("inst", None, ("row", "pitch")),
        check_vma=False,
    )
```

```python
import functools
import jax
import jax.numpy as jnp
from jax import lax
from jax.experimental import pallas as pl
from jax.experimental.pallas import tpu as pltpu
from jax.sharding import PartitionSpec as P

LANE = 128
COMP = 5
TERMS = 2 * COMP
PACK = 16
GROUP = 4
MESH = pl.DeviceIdType.MESH


def gathered(own, cell):
    low = cell & (LANE - 1)
    high = cell >> 7
    chunks = own.shape[1] * GROUP
    masks = [high == h for h in range(chunks)]
    values = []
    for b in range(COMP):
        found = None
        for h in range(chunks):
            row = own[b, h // GROUP, pl.ds(h % GROUP, 1), :]
            part = jnp.take_along_axis(
                jnp.broadcast_to(row, cell.shape), low, axis=1, mode="promise_in_bounds"
            )
            found = part if h == 0 else jnp.where(masks[h], part, found)
        values.append(found)
    return values


def applied(block, base, values):
    result = []
    for a in range(COMP):
        total = None
        for b in range(COMP):
            term = block(base + COMP * a + b) * values[b]
            total = term if total is None else total + term
        result.append(total)
    return result


def two_terms(value):
    first = value.astype(jnp.bfloat16).astype(jnp.float32)
    return first, value - first


def packed_row(row):
    return jnp.broadcast_to(row, (PACK, LANE)).astype(jnp.bfloat16)


def hot_tile(hot, place, cell_row, value):
    low = packed_row((cell_row & (LANE - 1)).astype(jnp.float32))
    for s in range(0, LANE, PACK):
        index = lax.broadcasted_iota(jnp.int32, (PACK, LANE), 0) + s
        index = index.astype(jnp.float32).astype(jnp.bfloat16)
        hot[s : s + PACK, place : place + LANE] = jnp.where(
            index == low, jnp.bfloat16(value), jnp.bfloat16(0)
        )


def chunk_mask(cell_row):
    index = lax.broadcasted_iota(jnp.int32, (PACK, LANE), 0)
    index = index.astype(jnp.float32).astype(jnp.bfloat16)
    return index == packed_row((cell_row >> 7).astype(jnp.float32))


def kernel(
    n_inst,
    n_row,
    n_pitch,
    tm_hbm,
    dir_hbm,
    vol_hbm,
    diag_hbm,
    face_hbm,
    left_hbm,
    right_hbm,
    bound_hbm,
    bcell_hbm,
    scell_hbm,
    out_ref,
    tm_ref,
    own,
    vol_line,
    vol,
    diag,
    face,
    left,
    right,
    bound,
    bcell,
    scell,
    dirs,
    ghost_out,
    ghost_in,
    flux_terms,
    bound_terms,
    rows,
    hot,
    acc,
    local_sem,
    inst_send,
    inst_recv,
    ghost_send,
    ghost_recv,
):
    t = lax.axis_index("inst")
    r = lax.axis_index("row")
    p = lax.axis_index("pitch")
    blocks = own.shape[1]
    chunks = blocks * GROUP
    f_tiles = left.shape[0]
    faces = f_tiles * LANE
    bounds = bcell.shape[1]
    b_tiles = bounds // LANE

    barrier = pltpu.get_barrier_semaphore()

    def greet(**place):
        pl.semaphore_signal(barrier, inc=1, device_id=place, device_id_type=MESH)

    up = lax.rem(p + 1, n_pitch)
    down = lax.rem(p + n_pitch - 1, n_pitch)
    greet(pitch=up)
    greet(pitch=down)

    @pl.when(r > 0)
    def _():
        greet(row=r - 1)

    @pl.when(r < n_row - 1)
    def _():
        greet(row=r + 1)

    for o in range(1, n_inst):
        greet(inst=lax.rem(t + o, n_inst))

    pairs = [
        (dir_hbm, own),
        (scell_hbm, scell),
        (bcell_hbm, bcell),
        (left_hbm, left),
        (right_hbm, right),
        (face_hbm, face),
        (bound_hbm, bound),
        (diag_hbm, diag),
        (vol_hbm, vol_line),
        (tm_hbm, tm_ref),
    ]
    copies = [
        pltpu.make_async_copy(a, b, local_sem.at[i]) for i, (a, b) in enumerate(pairs)
    ]
    for c in copies:
        c.start()

    for c in copies[0:3]:
        c.wait()
    inner = []
    for j in range(b_tiles):
        at = slice(j * LANE, (j + 1) * LANE)
        values = gathered(own, jnp.concatenate([scell[:, at], bcell[:, at]], axis=0))
        for b in range(COMP):
            ghost_out[j, pl.ds(b, GROUP, stride=8), :] = values[b][0:GROUP]
        inner.append([v[GROUP : 2 * GROUP] for v in values])

    greeted = 2 + n_inst - 1
    extra = jnp.where(r > 0, 1, 0) + jnp.where(r < n_row - 1, 1, 0)
    pl.semaphore_wait(barrier, greeted + extra)

    def ghost_copy(k, **place):
        opposite = k ^ 1
        return pltpu.make_async_remote_copy(
            src_ref=ghost_out.at[:, 8 * k : 8 * k + COMP],
            dst_ref=ghost_in.at[:, 8 * opposite : 8 * opposite + COMP],
            send_sem=ghost_send.at[k],
            recv_sem=ghost_recv.at[opposite],
            device_id=place,
            device_id_type=MESH,
        )

    to_down = ghost_copy(0, pitch=down)
    to_up = ghost_copy(1, pitch=up)
    to_down.start()
    to_up.start()

    @pl.when(r > 0)
    def _():
        ghost_copy(2, row=r - 1).start()

    @pl.when(r < n_row - 1)
    def _():
        ghost_copy(3, row=r + 1).start()

    sends = []
    for o in range(1, n_inst):
        c = pltpu.make_async_remote_copy(
            src_ref=dir_hbm,
            dst_ref=dirs.at[o],
            send_sem=inst_send.at[o],
            recv_sem=inst_recv.at[o],
            device_id={"inst": lax.rem(t + o, n_inst)},
            device_id_type=MESH,
        )
        c.start()
        sends.append(c)

    @pl.when(r == 0)
    def _():
        ghost_in[:, 16:24, :] = jnp.zeros((b_tiles, 8, LANE), jnp.float32)

    @pl.when(r == n_row - 1)
    def _():
        ghost_in[:, 24:32, :] = jnp.zeros((b_tiles, 8, LANE), jnp.float32)

    for c in copies[3:10]:
        c.wait()

    def product(start, size):
        return lax.dot_general(
            rows[:, start : start + size],
            hot[:, start : start + size],
            (((1,), (1,)), ((), ())),
            preferred_element_type=jnp.float32,
        )

    total = None
    for g in range(0, f_tiles, 8):
        block = lambda i, g=g: face[i, g : g + 8, :]
        cell_l = left[g : g + 8, :]
        cell_r = right[g : g + 8, :]
        one = applied(block, 0, gathered(own, cell_l))
        two = applied(block, COMP * COMP, gathered(own, cell_r))
        for a in range(COMP):
            first, rest = two_terms(one[a] + two[a])
            flux_terms[a, g : g + 8, :] = first
            flux_terms[COMP + a, g : g + 8, :] = rest
        for s in range(g, g + 8):
            place = 2 * s * LANE
            row_l = left[s : s + 1, :]
            row_r = right[s : s + 1, :]
            hot_tile(hot, place, row_l, 1.0)
            hot_tile(hot, place + LANE, row_r, -1.0)
            mask_l = chunk_mask(row_l)
            mask_r = chunk_mask(row_r)
            for a in range(TERMS):
                value = packed_row(flux_terms[a, s : s + 1, :])
                at = slice(a * PACK, (a + 1) * PACK)
                zero = jnp.bfloat16(0)
                rows[at, place : place + LANE] = jnp.where(mask_l, value, zero)
                rows[at, place + LANE : place + 2 * LANE] = jnp.where(mask_r, value, zero)
        part = product(2 * g * LANE, 16 * LANE)
        total = part if total is None else total + part
    acc[...] = total

    def boundary_place(j, k):
        pair = 1 - k // 2
        return 2 * faces + 2 * pair * bounds + (2 * j + k % 2) * LANE

    inner_flux = []
    for j in range(b_tiles):
        at = slice(j * LANE, (j + 1) * LANE)
        inner_flux.append(applied(lambda i, at=at: bound[i, :, at], 0, inner[j]))
        for k in range(GROUP):
            hot_tile(hot, boundary_place(j, k), bcell[k : k + 1, at], 1.0)
    for h in range(chunks):
        vol[h // GROUP, pl.ds(h % GROUP, 1), :] = vol_line[
            h * LANE : (h + 1) * LANE
        ].reshape(1, LANE)

    for q in range(blocks):
        local = applied(lambda i, q=q: diag[i, q], 0, [own[b, q] for b in range(COMP)])
        for a in range(COMP):
            out_ref[a, q] = local[a] + (tm_ref[t, t] * own[a, q]) * vol[q]

    def boundary(start):
        for j in range(b_tiles):
            at = slice(j * LANE, (j + 1) * LANE)
            outer = [
                ghost_in[j, pl.ds(8 * start + b, 2, stride=8), :] for b in range(COMP)
            ]
            block = lambda i, at=at: bound[i, start : start + 2, at]
            flux = applied(block, COMP * COMP, outer)
            for a in range(COMP):
                first, rest = two_terms(inner_flux[j][a][start : start + 2] + flux[a])
                bound_terms[a, j, start : start + 2, :] = first
                bound_terms[COMP + a, j, start : start + 2, :] = rest
            for k in range(start, start + 2):
                place = boundary_place(j, k)
                mask = chunk_mask(bcell[k : k + 1, at])
                for a in range(TERMS):
                    value = packed_row(bound_terms[a, j, pl.ds(k, 1), :])
                    rows[a * PACK : (a + 1) * PACK, place : place + LANE] = jnp.where(
                        mask, value, jnp.bfloat16(0)
                    )

    @pl.when(r > 0)
    def _():
        ghost_copy(2, row=r - 1).wait_send()
        half = ghost_in.at[:, 16 : 16 + COMP]
        pltpu.make_async_copy(half, half, ghost_recv.at[2]).wait()

    @pl.when(r < n_row - 1)
    def _():
        ghost_copy(3, row=r + 1).wait_send()
        half = ghost_in.at[:, 24 : 24 + COMP]
        pltpu.make_async_copy(half, half, ghost_recv.at[3]).wait()

    boundary(2)
    acc[...] = acc[...] + product(2 * faces, 2 * bounds)

    for c in sends:
        c.wait()
    weights = [tm_ref[t, lax.rem(t + n_inst - o, n_inst)] for o in range(1, n_inst)]
    for q in range(blocks):
        for a in range(COMP):
            mixed = None
            for o in range(1, n_inst):
                term = weights[o - 1] * dirs[o, a, q]
                mixed = term if mixed is None else mixed + term
            at = a * PACK + q * GROUP
            both = acc[at : at + GROUP, :]
            at = at + COMP * PACK
            both = both + acc[at : at + GROUP, :]
            out_ref[a, q] = out_ref[a, q] + mixed * vol[q] + both

    to_down.wait()
    to_up.wait()
    boundary(0)
    acc[...] = product(2 * faces + 2 * bounds, 2 * bounds)
    for q in range(blocks):
        for a in range(COMP):
            at = a * PACK + q * GROUP
            both = acc[at : at + GROUP, :]
            at = at + COMP * PACK
            out_ref[a, q] = out_ref[a, q] + (both + acc[at : at + GROUP, :])


def per_device(
    direction,
    time_matrix,
    volume,
    diag_jac,
    face_jac,
    face_left,
    face_right,
    bound_jac,
    bound_cell,
    send_cell,
):
    n_inst = lax.axis_size("inst")
    n_row = lax.axis_size("row")
    n_pitch = lax.axis_size("pitch")
    cells = direction.shape[2]
    faces = face_left.shape[0]
    bounds = bound_cell.shape[1]
    blocks = cells // (GROUP * LANE)
    f_tiles = faces // LANE
    b_tiles = bounds // LANE
    width = 2 * faces + 4 * bounds
    f32, i32, bf16 = jnp.float32, jnp.int32, jnp.bfloat16
    cell_view = (blocks, GROUP, LANE)
    hbm = pl.BlockSpec(memory_space=pl.ANY)
    result = pl.pallas_call(
        functools.partial(kernel, n_inst, n_row, n_pitch),
        out_shape=pltpu.VMEM((COMP, *cell_view), f32),
        in_specs=[hbm] * 10,
        out_specs=pl.BlockSpec(memory_space=pltpu.VMEM),
        scratch_shapes=[
            pltpu.SMEM((n_inst, n_inst), f32),
            pltpu.VMEM((COMP, *cell_view), f32),
            pltpu.VMEM((cells,), f32),
            pltpu.VMEM(cell_view, f32),
            pltpu.VMEM((25, *cell_view), f32),
            pltpu.VMEM((50, f_tiles, LANE), f32),
            pltpu.VMEM((f_tiles, LANE), i32),
            pltpu.VMEM((f_tiles, LANE), i32),
            pltpu.VMEM((50, 4, bounds), f32),
            pltpu.VMEM((4, bounds), i32),
            pltpu.VMEM((4, bounds), i32),
            pltpu.VMEM((n_inst, COMP, *cell_view), f32),
            pltpu.VMEM((b_tiles, 32, LANE), f32),
            pltpu.VMEM((b_tiles, 32, LANE), f32),
            pltpu.VMEM((TERMS, f_tiles, LANE), f32),
            pltpu.VMEM((TERMS, b_tiles, GROUP, LANE), f32),
            pltpu.VMEM((TERMS * PACK, width), bf16),
            pltpu.VMEM((LANE, width), bf16),
            pltpu.VMEM((TERMS * PACK, LANE), f32),
            pltpu.SemaphoreType.DMA((10,)),
            pltpu.SemaphoreType.DMA((n_inst,)),
            pltpu.SemaphoreType.DMA((n_inst,)),
            pltpu.SemaphoreType.DMA((4,)),
            pltpu.SemaphoreType.DMA((4,)),
        ],
        compiler_params=pltpu.CompilerParams(collective_id=0, has_side_effects=True),
    )(
        time_matrix,
        direction[0].reshape(COMP, *cell_view),
        volume,
        diag_jac[0].reshape(25, *cell_view),
        face_jac[0].reshape(50, f_tiles, LANE),
        face_left.reshape(f_tiles, LANE),
        face_right.reshape(f_tiles, LANE),
        bound_jac[0].transpose(1, 0, 2),
        bound_cell,
        send_cell,
    )
    return result.reshape(1, COMP, cells)


def solution(mesh):
    return jax.shard_map(
        per_device,
        mesh=mesh,
        in_specs=(
            P("inst", None, ("row", "pitch")),
            P(),
            P(("row", "pitch")),
            P("inst", None, ("row", "pitch")),
            P("inst", None, ("row", "pitch")),
            P(("row", "pitch")),
            P(("row", "pitch")),
            P("inst", None, None, ("row", "pitch")),
            P(None, ("row", "pitch")),
            P(None, ("row", "pitch")),
        ),
        out_specs=P("inst", None, ("row", "pitch")),
        check_vma=False,
    )
```

```python
import functools
import jax
import jax.numpy as jnp
from jax import lax
from jax.experimental import pallas as pl
from jax.experimental.pallas import tpu as pltpu
from jax.sharding import PartitionSpec as P

LANE = 128
COMP = 5
TERMS = 2 * COMP
PACK = 16
GROUP = 4
MESH = pl.DeviceIdType.MESH


def gathered(own, cell):
    low = cell & (LANE - 1)
    high = cell >> 7
    chunks = own.shape[1] * GROUP
    masks = [high == h for h in range(chunks)]
    values = []
    for b in range(COMP):
        found = None
        for h in range(chunks):
            row = own[b, h // GROUP, pl.ds(h % GROUP, 1), :]
            part = jnp.take_along_axis(
                jnp.broadcast_to(row, cell.shape), low, axis=1, mode="promise_in_bounds"
            )
            found = part if h == 0 else jnp.where(masks[h], part, found)
        values.append(found)
    return values


def applied(block, base, values):
    result = []
    for a in range(COMP):
        total = None
        for b in range(COMP):
            term = block(base + COMP * a + b) * values[b]
            total = term if total is None else total + term
        result.append(total)
    return result


def two_terms(value):
    first = value.astype(jnp.bfloat16).astype(jnp.float32)
    return first, value - first


def packed_row(row):
    return jnp.broadcast_to(row, (PACK, LANE)).astype(jnp.bfloat16)


def hot_tile(hot, place, cell_row, value):
    low = packed_row((cell_row & (LANE - 1)).astype(jnp.float32))
    for s in range(0, LANE, PACK):
        index = lax.broadcasted_iota(jnp.int32, (PACK, LANE), 0) + s
        index = index.astype(jnp.float32).astype(jnp.bfloat16)
        hot[s : s + PACK, place : place + LANE] = jnp.where(
            index == low, jnp.bfloat16(value), jnp.bfloat16(0)
        )


def chunk_mask(cell_row):
    index = lax.broadcasted_iota(jnp.int32, (PACK, LANE), 0)
    index = index.astype(jnp.float32).astype(jnp.bfloat16)
    return index == packed_row((cell_row >> 7).astype(jnp.float32))


def kernel(
    n_inst,
    n_row,
    n_pitch,
    tm_hbm,
    dir_hbm,
    vol_hbm,
    diag_hbm,
    face_hbm,
    left_hbm,
    right_hbm,
    bound_hbm,
    bcell_hbm,
    scell_hbm,
    out_ref,
    tm_ref,
    own,
    vol_line,
    vol,
    diag,
    face,
    left,
    right,
    bound,
    bcell,
    scell,
    dirs,
    ghost_out,
    ghost_in,
    flux_terms,
    bound_terms,
    rows,
    hot,
    acc,
    local_sem,
    inst_send,
    inst_recv,
    ghost_send,
    ghost_recv,
):
    t = lax.axis_index("inst")
    r = lax.axis_index("row")
    p = lax.axis_index("pitch")
    blocks = own.shape[1]
    chunks = blocks * GROUP
    f_tiles = left.shape[0]
    faces = f_tiles * LANE
    bounds = bcell.shape[1]
    b_tiles = bounds // LANE

    barrier = pltpu.get_barrier_semaphore()

    def greet(**place):
        pl.semaphore_signal(barrier, inc=1, device_id=place, device_id_type=MESH)

    up = lax.rem(p + 1, n_pitch)
    down = lax.rem(p + n_pitch - 1, n_pitch)
    greet(pitch=up)
    greet(pitch=down)

    @pl.when(r > 0)
    def _():
        greet(row=r - 1)

    @pl.when(r < n_row - 1)
    def _():
        greet(row=r + 1)

    for o in range(1, n_inst):
        greet(inst=lax.rem(t + o, n_inst))

    pairs = [
        (dir_hbm, own),
        (scell_hbm, scell),
        (bcell_hbm, bcell),
        (left_hbm, left),
        (right_hbm, right),
        (face_hbm, face),
        (bound_hbm, bound),
        (diag_hbm, diag),
        (vol_hbm, vol_line),
        (tm_hbm, tm_ref),
    ]
    copies = [
        pltpu.make_async_copy(a, b, local_sem.at[i]) for i, (a, b) in enumerate(pairs)
    ]
    for c in copies:
        c.start()

    for c in copies[0:3]:
        c.wait()
    inner = []
    for j in range(b_tiles):
        at = slice(j * LANE, (j + 1) * LANE)
        values = gathered(own, jnp.concatenate([scell[:, at], bcell[:, at]], axis=0))
        for b in range(COMP):
            ghost_out[j, pl.ds(b, GROUP, stride=8), :] = values[b][0:GROUP]
        inner.append([v[GROUP : 2 * GROUP] for v in values])

    greeted = 2 + n_inst - 1
    extra = jnp.where(r > 0, 1, 0) + jnp.where(r < n_row - 1, 1, 0)
    pl.semaphore_wait(barrier, greeted + extra)

    def ghost_copy(k, **place):
        opposite = k ^ 1
        return pltpu.make_async_remote_copy(
            src_ref=ghost_out.at[:, 8 * k : 8 * k + COMP],
            dst_ref=ghost_in.at[:, 8 * opposite : 8 * opposite + COMP],
            send_sem=ghost_send.at[k],
            recv_sem=ghost_recv.at[opposite],
            device_id=place,
            device_id_type=MESH,
        )

    to_down = ghost_copy(0, pitch=down)
    to_up = ghost_copy(1, pitch=up)
    to_down.start()
    to_up.start()

    @pl.when(r > 0)
    def _():
        ghost_copy(2, row=r - 1).start()

    @pl.when(r < n_row - 1)
    def _():
        ghost_copy(3, row=r + 1).start()

    sends = []
    for o in range(1, n_inst):
        c = pltpu.make_async_remote_copy(
            src_ref=own,
            dst_ref=dirs.at[o],
            send_sem=inst_send.at[o],
            recv_sem=inst_recv.at[o],
            device_id={"inst": lax.rem(t + o, n_inst)},
            device_id_type=MESH,
        )
        c.start()
        sends.append(c)

    @pl.when(r == 0)
    def _():
        ghost_in[:, 16:24, :] = jnp.zeros((b_tiles, 8, LANE), jnp.float32)

    @pl.when(r == n_row - 1)
    def _():
        ghost_in[:, 24:32, :] = jnp.zeros((b_tiles, 8, LANE), jnp.float32)

    for c in copies[3:10]:
        c.wait()

    def product(start, size):
        return lax.dot_general(
            rows[:, start : start + size],
            hot[:, start : start + size],
            (((1,), (1,)), ((), ())),
            preferred_element_type=jnp.float32,
        )

    total = None
    for g in range(0, f_tiles, 8):
        block = lambda i, g=g: face[i, g : g + 8, :]
        cell_l = left[g : g + 8, :]
        cell_r = right[g : g + 8, :]
        one = applied(block, 0, gathered(own, cell_l))
        two = applied(block, COMP * COMP, gathered(own, cell_r))
        for a in range(COMP):
            first, rest = two_terms(one[a] + two[a])
            flux_terms[a, g : g + 8, :] = first
            flux_terms[COMP + a, g : g + 8, :] = rest
        for s in range(g, g + 8):
            place = 2 * s * LANE
            row_l = left[s : s + 1, :]
            row_r = right[s : s + 1, :]
            hot_tile(hot, place, row_l, 1.0)
            hot_tile(hot, place + LANE, row_r, -1.0)
            mask_l = chunk_mask(row_l)
            mask_r = chunk_mask(row_r)
            for a in range(TERMS):
                value = packed_row(flux_terms[a, s : s + 1, :])
                at = slice(a * PACK, (a + 1) * PACK)
                zero = jnp.bfloat16(0)
                rows[at, place : place + LANE] = jnp.where(mask_l, value, zero)
                rows[at, place + LANE : place + 2 * LANE] = jnp.where(mask_r, value, zero)
        part = product(2 * g * LANE, 16 * LANE)
        total = part if total is None else total + part
    acc[...] = total

    def boundary_place(j, k):
        pair = 1 - k // 2
        return 2 * faces + 2 * pair * bounds + (2 * j + k % 2) * LANE

    inner_flux = []
    for j in range(b_tiles):
        at = slice(j * LANE, (j + 1) * LANE)
        inner_flux.append(applied(lambda i, at=at: bound[i, :, at], 0, inner[j]))
        for k in range(GROUP):
            hot_tile(hot, boundary_place(j, k), bcell[k : k + 1, at], 1.0)
    for h in range(chunks):
        vol[h // GROUP, pl.ds(h % GROUP, 1), :] = vol_line[
            h * LANE : (h + 1) * LANE
        ].reshape(1, LANE)

    for q in range(blocks):
        local = applied(lambda i, q=q: diag[i, q], 0, [own[b, q] for b in range(COMP)])
        for a in range(COMP):
            out_ref[a, q] = local[a] + (tm_ref[t, t] * own[a, q]) * vol[q]

    def boundary(start):
        for j in range(b_tiles):
            at = slice(j * LANE, (j + 1) * LANE)
            outer = [
                ghost_in[j, pl.ds(8 * start + b, 2, stride=8), :] for b in range(COMP)
            ]
            block = lambda i, at=at: bound[i, start : start + 2, at]
            flux = applied(block, COMP * COMP, outer)
            for a in range(COMP):
                first, rest = two_terms(inner_flux[j][a][start : start + 2] + flux[a])
                bound_terms[a, j, start : start + 2, :] = first
                bound_terms[COMP + a, j, start : start + 2, :] = rest
            for k in range(start, start + 2):
                place = boundary_place(j, k)
                mask = chunk_mask(bcell[k : k + 1, at])
                for a in range(TERMS):
                    value = packed_row(bound_terms[a, j, pl.ds(k, 1), :])
                    rows[a * PACK : (a + 1) * PACK, place : place + LANE] = jnp.where(
                        mask, value, jnp.bfloat16(0)
                    )

    @pl.when(r > 0)
    def _():
        ghost_copy(2, row=r - 1).wait_send()
        half = ghost_in.at[:, 16 : 16 + COMP]
        pltpu.make_async_copy(half, half, ghost_recv.at[2]).wait()

    @pl.when(r < n_row - 1)
    def _():
        ghost_copy(3, row=r + 1).wait_send()
        half = ghost_in.at[:, 24 : 24 + COMP]
        pltpu.make_async_copy(half, half, ghost_recv.at[3]).wait()

    boundary(2)
    acc[...] = acc[...] + product(2 * faces, 2 * bounds)

    for c in sends:
        c.wait()
    weights = [tm_ref[t, lax.rem(t + n_inst - o, n_inst)] for o in range(1, n_inst)]
    for q in range(blocks):
        for a in range(COMP):
            mixed = None
            for o in range(1, n_inst):
                term = weights[o - 1] * dirs[o, a, q]
                mixed = term if mixed is None else mixed + term
            at = a * PACK + q * GROUP
            both = acc[at : at + GROUP, :]
            at = at + COMP * PACK
            both = both + acc[at : at + GROUP, :]
            out_ref[a, q] = out_ref[a, q] + mixed * vol[q] + both

    to_down.wait()
    to_up.wait()
    boundary(0)
    acc[...] = product(2 * faces + 2 * bounds, 2 * bounds)
    for q in range(blocks):
        for a in range(COMP):
            at = a * PACK + q * GROUP
            both = acc[at : at + GROUP, :]
            at = at + COMP * PACK
            out_ref[a, q] = out_ref[a, q] + (both + acc[at : at + GROUP, :])


def per_device(
    direction,
    time_matrix,
    volume,
    diag_jac,
    face_jac,
    face_left,
    face_right,
    bound_jac,
    bound_cell,
    send_cell,
):
    n_inst = lax.axis_size("inst")
    n_row = lax.axis_size("row")
    n_pitch = lax.axis_size("pitch")
    cells = direction.shape[2]
    faces = face_left.shape[0]
    bounds = bound_cell.shape[1]
    blocks = cells // (GROUP * LANE)
    f_tiles = faces // LANE
    b_tiles = bounds // LANE
    width = 2 * faces + 4 * bounds
    f32, i32, bf16 = jnp.float32, jnp.int32, jnp.bfloat16
    cell_view = (blocks, GROUP, LANE)
    hbm = pl.BlockSpec(memory_space=pl.ANY)
    result = pl.pallas_call(
        functools.partial(kernel, n_inst, n_row, n_pitch),
        out_shape=pltpu.VMEM((COMP, *cell_view), f32),
        in_specs=[hbm] * 10,
        out_specs=pl.BlockSpec(memory_space=pltpu.VMEM),
        scratch_shapes=[
            pltpu.SMEM((n_inst, n_inst), f32),
            pltpu.VMEM((COMP, *cell_view), f32),
            pltpu.VMEM((cells,), f32),
            pltpu.VMEM(cell_view, f32),
            pltpu.VMEM((25, *cell_view), f32),
            pltpu.VMEM((50, f_tiles, LANE), f32),
            pltpu.VMEM((f_tiles, LANE), i32),
            pltpu.VMEM((f_tiles, LANE), i32),
            pltpu.VMEM((50, 4, bounds), f32),
            pltpu.VMEM((4, bounds), i32),
            pltpu.VMEM((4, bounds), i32),
            pltpu.VMEM((n_inst, COMP, *cell_view), f32),
            pltpu.VMEM((b_tiles, 32, LANE), f32),
            pltpu.VMEM((b_tiles, 32, LANE), f32),
            pltpu.VMEM((TERMS, f_tiles, LANE), f32),
            pltpu.VMEM((TERMS, b_tiles, GROUP, LANE), f32),
            pltpu.VMEM((TERMS * PACK, width), bf16),
            pltpu.VMEM((LANE, width), bf16),
            pltpu.VMEM((TERMS * PACK, LANE), f32),
            pltpu.SemaphoreType.DMA((10,)),
            pltpu.SemaphoreType.DMA((n_inst,)),
            pltpu.SemaphoreType.DMA((n_inst,)),
            pltpu.SemaphoreType.DMA((4,)),
            pltpu.SemaphoreType.DMA((4,)),
        ],
        compiler_params=pltpu.CompilerParams(collective_id=0, has_side_effects=True),
    )(
        time_matrix,
        direction[0].reshape(COMP, *cell_view),
        volume,
        diag_jac[0].reshape(25, *cell_view),
        face_jac[0].reshape(50, f_tiles, LANE),
        face_left.reshape(f_tiles, LANE),
        face_right.reshape(f_tiles, LANE),
        bound_jac[0].transpose(1, 0, 2),
        bound_cell,
        send_cell,
    )
    return result.reshape(1, COMP, cells)


def solution(mesh):
    return jax.shard_map(
        per_device,
        mesh=mesh,
        in_specs=(
            P("inst", None, ("row", "pitch")),
            P(),
            P(("row", "pitch")),
            P("inst", None, ("row", "pitch")),
            P("inst", None, ("row", "pitch")),
            P(("row", "pitch")),
            P(("row", "pitch")),
            P("inst", None, None, ("row", "pitch")),
            P(None, ("row", "pitch")),
            P(None, ("row", "pitch")),
        ),
        out_specs=P("inst", None, ("row", "pitch")),
        check_vma=False,
    )
```
